32 devices in a mesh: pitch: 2 (over core), axial: 4 (over y, x), span: 4 (over z).
Axes of the slice: x: 2, y: 2, z: 4, core: 2. Of those that a mesh axis runs over, the one named last changes fastest.
Arguments:
- state: float32 [5, 16, 128, 512], P(None, 'pitch', 'axial', 'span'), as said below
- coeffs: float32 [2, 4, 5, 128, 512], P(None, None, None, 'axial', 'span'), may hold values from -3 to 3
- lag_shift: int32 [1], replicated, may hold values from 0 to 63
- harmonics: int32 [512], P('span'), may hold values from 1 to 4
Outputs:
- new_state: float32 [5, 16, 128, 512], P(None, 'pitch', 'axial', 'span')
The draws below stay inside these ranges and needn't reach their ends.
Inputs may be any that keep to these rules, and one draw needn't show every extreme that they name: `state`: density lies in 0.8 to 1.25, momenta within -1.5 to 1.5, total energy within 1.6 to 3.4.
All inputs are finite; a program needn't handle non-finite values.
Results may differ from the reference program's by a relative error of at most 0.0001.
Values sent between devices are 32-bit elements; how exact they have to be, the bound alone decides.
A program may use at most 64 MiB of HBM per device.

```python
import math
import jax
import jax.numpy as jnp

FIELDS = 5
HARM_MAX = 4
PERIOD_SAMPLES = 64
NPITCH = 16
NAXIAL = 128
NSPAN = 512
DIFF_NUMBER = 4


def draw_state(key, part):
    keys = jax.random.split(key, 3)
    shape_cells = (NPITCH, NAXIAL, NSPAN)
    density = jax.random.uniform(keys[0], shape_cells, jnp.float32, 0.8, 1.25)
    momentum = 0.5 * jax.random.truncated_normal(keys[1], -3.0, 3.0, (3,) + shape_cells, jnp.float32)
    energy = 2.5 + 0.3 * jax.random.truncated_normal(keys[2], -3.0, 3.0, shape_cells, jnp.float32)
    return jnp.concatenate([density[None], momentum, energy[None]], axis=0)


def plant(values, key, smallest, top_value):
    longest = values.shape.index(max(values.shape))
    spots = []
    for shift in (0, 1):
        where = [jax.random.randint(jax.random.fold_in(key, axis), (), 0, length) for axis, length in enumerate(values.shape)]
        where[longest] = (where[longest] + shift) % values.shape[longest]
        spots.append(tuple(where))
    return values.at[spots[0]].set(smallest).at[spots[1]].set(top_value)


def level_of(own_key, extent, cuts, smallest, high):
    factor_of = 1.0
    for dim, blocks in cuts:
        draws = jax.random.uniform(jax.random.fold_in(jax.random.fold_in(own_key, 6), dim), (blocks,), jnp.float32, smallest / len(cuts), high / len(cuts))
        factor_of = factor_of * jnp.repeat(jnp.exp(draws), extent[dim] // blocks).reshape((-1,) + (1,) * (len(extent) - 1 - dim))
    return factor_of


def gaussian(key, extent, scale, bound, pieces=(), kind=jnp.bfloat16):
    values = jax.random.normal(key, extent, jnp.float32) * scale
    if len(pieces) > 0:
        values = level_of(key, extent, pieces, -0.22, 0.18) * values
    return jnp.clip(values, min=-bound, max=bound).astype(kind)


def setup_inputs(seed: int = 0) -> dict:
    key_of = jax.random.split(jax.random.key(seed), 5)
    return {
        "state": draw_state(jax.random.fold_in(key_of[4], 71), 0),
        "coeffs": gaussian(key_of[1], (2, HARM_MAX, FIELDS, NAXIAL, NSPAN), 0.5, 3.0, ((3, 4), (4, 4)), jnp.float32),
        "lag_shift": jax.random.randint(key_of[2], (1,), 0, PERIOD_SAMPLES).astype(jnp.int32),
        "harmonics": plant(jax.random.randint(key_of[3], (NSPAN,), 1, HARM_MAX + 1), jax.random.fold_in(key_of[3], 1), 1, HARM_MAX).astype(jnp.int32),
    }


HEAT_RATIO_GAS = 1.4
STEP_RATE = 0.25
DAMPING = 0.5
STENCIL = (1.0, -8.0, 28.0, -56.0, 70.0, -56.0, 28.0, -8.0, 1.0)


def pitch_flux(state):
    density = state[0]
    speed = state[2] / density
    kinetic = 0.5 * (state[1] * state[1] + state[2] * state[2] + state[3] * state[3]) / density
    pressure = (HEAT_RATIO_GAS - 1.0) * (state[4] - kinetic)
    return jnp.stack([state[2], state[1] * speed, state[2] * speed + pressure, state[3] * speed, (state[4] + pressure) * speed])


def seam_jump(coeffs, lag_shift, harmonics):
    order = jnp.arange(HARM_MAX)
    phase = (2.0 * math.pi / PERIOD_SAMPLES) * (order + 1).astype(jnp.float32) * lag_shift[0].astype(jnp.float32)
    active = (order[:, None] < harmonics[None, :]).astype(jnp.float32)
    cosine = active * jnp.cos(phase)[:, None]
    sine = active * jnp.sin(phase)[:, None]
    first = jnp.sum(cosine[:, None, None, :] * coeffs[0], axis=0)
    second = jnp.sum(sine[:, None, None, :] * coeffs[1], axis=0)
    return first + second


def damping_from(extended, naxial, nspan):
    along = jnp.zeros_like(extended[:, :, 4:4 + naxial, 4:4 + nspan])
    across = jnp.zeros_like(along)
    for displacement in range(9):
        along = along + STENCIL[displacement] * extended[:, :, displacement:displacement + naxial, 4:4 + nspan]
        across = across + STENCIL[displacement] * extended[:, :, 4:4 + naxial, displacement:displacement + nspan]
    return (along + across) / 256.0


def cyclic_tridiagonal_solve(values, operator_symbol):
    results = []
    for field in range(FIELDS):
        spectrum = jnp.fft.fft(values[field], axis=0) / operator_symbol
        results.append(jnp.real(jnp.fft.ifft(spectrum, axis=0)).astype(jnp.float32))
    return jnp.stack(results)


def reference(state, coeffs, lag_shift, harmonics):
    flux = pitch_flux(state)
    jump = seam_jump(coeffs, lag_shift, harmonics)
    rhs = 0.75 * (jnp.roll(flux, -1, axis=1) - jnp.roll(flux, 1, axis=1))
    rhs = rhs.at[:, 0].add(0.75 * jump)
    rhs = rhs.at[:, -1].add(0.75 * jump)
    wave = (2.0 * math.pi / NPITCH) * jnp.arange(NPITCH).astype(jnp.float32)
    compact_symbol = (1.0 + 0.5 * jnp.cos(wave)).reshape(NPITCH, 1, 1)
    diffusion = float(DIFF_NUMBER)
    relax_symbol = (1.0 + 2.0 * diffusion * (1.0 - jnp.cos(wave))).reshape(NPITCH, 1, 1)
    deriv = cyclic_tridiagonal_solve(rhs, compact_symbol)
    smoothed_increment = cyclic_tridiagonal_solve(state, relax_symbol)
    extended = jnp.pad(state, ((0, 0), (0, 0), (4, 4), (4, 4)))
    damp = damping_from(extended, state.shape[2], state.shape[3])
    return smoothed_increment - STEP_RATE * deriv - DAMPING * damp
```

```python
import functools
import math

import jax
import jax.numpy as jnp
from jax import lax
from jax.experimental import pallas as pl
from jax.experimental.pallas import tpu as pltpu
from jax.sharding import PartitionSpec as P

PERIOD_SAMPLES = 64
HEAT_RATIO_GAS = 1.4
STEP_RATE = 0.25
DAMPING = 0.5
EDGE = (1.0, -8.0, 28.0, -56.0)
MESH = pl.DeviceIdType.MESH


def line_root(main, side):
    root = (-main + math.sqrt(main * main - 4.0 * side * side)) / (2.0 * side)
    return root, 1.0 / (main + 2.0 * side * root)


def pick(position, values):
    chosen = jnp.float32(values[-1])
    for index in range(len(values) - 1):
        chosen = jnp.where(position == index, jnp.float32(values[index]), chosen)
    return chosen


def kernel(
    sizes,
    lag_ref,
    harm_ref,
    state_hbm,
    coef_hbm,
    out_ref,
    u,
    co,
    flux,
    sums,
    got_sums,
    ax_tail,
    ax_head,
    got_tail,
    got_head,
    sp_own,
    got_left,
    got_right,
    waves,
    local_sem,
    send_sem,
    recv_sem,
):
    npitch, naxial, nspan = sizes
    fields, cells, rows, _ = u.shape
    tiles = rows // 8
    harm_max = co.shape[1]
    total = cells * npitch
    diffusion = float(total * total // 64)
    r, r_scale = line_root(1.0, 0.25)
    q, q_scale = line_root(1.0 + 2.0 * diffusion, -diffusion)
    pitch, axial, span = (lax.axis_index(name) for name in ("pitch", "axial", "span"))

    state_copy = pltpu.make_async_copy(state_hbm, u, local_sem.at[0])
    coef_copy = pltpu.make_async_copy(coef_hbm, co, local_sem.at[1])
    state_copy.start()

    barrier = pltpu.get_barrier_semaphore()

    def greet(**where):
        pl.semaphore_signal(barrier, inc=1, device_id=where, device_id_type=MESH)

    has_up, has_down = axial > 0, axial < naxial - 1
    has_left, has_right = span > 0, span < nspan - 1

    @pl.when(has_up)
    def _():
        greet(axial=axial - 1)

    @pl.when(has_down)
    def _():
        greet(axial=axial + 1)

    @pl.when(has_left)
    def _():
        greet(span=span - 1)

    @pl.when(has_right)
    def _():
        greet(span=span + 1)

    for step in range(1, npitch):
        greet(pitch=lax.rem(pitch + step, npitch))
    coef_copy.start()

    row = lax.broadcasted_iota(jnp.int32, (8, 128), 0)
    lane = lax.broadcasted_iota(jnp.int32, (8, 128), 1)
    group = lane // 8
    low_rows = row < 4

    state_copy.wait()

    def pack_axial(f, carry):
        for k in range(cells // 2):
            a, b = u[f, 2 * k, rows - 8 :, :], u[f, 2 * k + 1, rows - 8 :, :]
            ax_tail[f, k] = jnp.where(low_rows, pltpu.roll(a, 4, 0), b)
            a, b = u[f, 2 * k, :8, :], u[f, 2 * k + 1, :8, :]
            ax_head[f, k] = jnp.where(low_rows, a, pltpu.roll(b, 4, 0))
        return carry

    lax.fori_loop(0, fields, pack_axial, 0)

    neighbours = npitch - 1
    for flag in (has_up, has_down, has_left, has_right):
        neighbours = neighbours + jnp.where(flag, 1, 0)
    pl.semaphore_wait(barrier, neighbours)

    def remote(src, dst, slot, **where):
        return pltpu.make_async_remote_copy(
            src_ref=src,
            dst_ref=dst,
            send_sem=send_sem.at[slot],
            recv_sem=recv_sem.at[slot],
            device_id=where,
            device_id_type=MESH,
        )

    down_copy = remote(ax_tail, got_tail, 0, axial=axial + 1)
    up_copy = remote(ax_head, got_head, 1, axial=axial - 1)
    right_copy = remote(sp_own, got_left, 2, span=span + 1)
    left_copy = remote(sp_own, got_right, 3, span=span - 1)

    def when(flag, action):
        @pl.when(flag)
        def _():
            action()

    def clear(ref):
        ref[...] = jnp.zeros_like(ref)

    when(has_down, down_copy.start)
    when(has_up, up_copy.start)

    half = cells // (sp_own.shape[1])

    def pack_span(f, carry):
        for g in range(sp_own.shape[1]):
            packed = jnp.zeros((8, 128), jnp.float32)
            for k in range(16):
                tile = u[f, g * half + k // tiles, (k % tiles) * 8 : (k % tiles) * 8 + 8, :]
                packed = jnp.where(group == k, pltpu.roll(tile, (8 * k + 4) % 128, 1), packed)
            sp_own[f, g] = packed
        return carry

    lax.fori_loop(0, fields, pack_span, 0)
    when(has_right, right_copy.start)
    when(has_left, left_copy.start)

    def flux_tile(t, carry):
        at = pl.ds(pl.multiple_of(t * 8, 8), 8)
        parts = [None] * 4
        for i in range(cells):
            cell = [u[f, i, at, :] for f in range(fields)]
            inverse = 1.0 / cell[0]
            speed = cell[2] * inverse
            kinetic = 0.5 * (cell[1] * cell[1] + cell[2] * cell[2] + cell[3] * cell[3]) * inverse
            pressure = (HEAT_RATIO_GAS - 1.0) * (cell[4] - kinetic)
            values = [
                cell[2],
                cell[1] * speed,
                cell[2] * speed + pressure,
                cell[3] * speed,
                (cell[4] + pressure) * speed,
            ]
            for f in range(fields):
                flux[f, i, at, :] = values[f]
            if i == 0:
                parts = [list(values), list(values), list(cell), list(cell)]
            else:
                for f in range(fields):
                    parts[0][f] = r * parts[0][f] + values[f]
                    parts[1][f] = parts[1][f] + (r**i) * values[f]
                    parts[2][f] = q * parts[2][f] + cell[f]
                    parts[3][f] = parts[3][f] + (q**i) * cell[f]
        for s in range(4):
            for f in range(fields):
                sums[s, f, at, :] = parts[s][f]
        return carry

    lax.fori_loop(0, tiles, flux_tile, 0)

    sum_copies = [
        remote(sums, got_sums.at[step - 1], 3 + step, pitch=lax.rem(pitch + step, npitch))
        for step in range(1, npitch)
    ]
    for copy in sum_copies:
        copy.start()

    when(jnp.logical_not(has_up), lambda: clear(got_tail))
    when(jnp.logical_not(has_down), lambda: clear(got_head))
    when(jnp.logical_not(has_left), lambda: clear(got_left))
    when(jnp.logical_not(has_right), lambda: clear(got_right))

    weight = -DAMPING / 256.0

    def damp_field(f, carry):
        for i in range(cells):
            x = u[f, i]
            result = (140.0 * weight) * x
            for o, c in ((1, -56.0), (2, 28.0), (3, -8.0), (4, 1.0)):
                pair = (pltpu.roll(x, o, 0) + pltpu.roll(x, rows - o, 0)) + (
                    pltpu.roll(x, o, 1) + pltpu.roll(x, 128 - o, 1)
                )
                result = result + (c * weight) * pair
            out_ref[f, i] = result
        return carry

    lax.fori_loop(0, fields, damp_field, 0)

    order = row.astype(jnp.float32) + 1.0
    phase = (2.0 * math.pi / PERIOD_SAMPLES) * order * lag_ref[0].astype(jnp.float32)
    active = row < harm_ref[...]
    waves[0] = jnp.where(active, jnp.cos(phase), 0.0)
    waves[1] = jnp.where(active, jnp.sin(phase), 0.0)
    near_first = pick(pitch, [r ** (cells * p) for p in range(npitch)])
    near_last = pick(pitch, [r ** (cells * (npitch - 1 - p)) for p in range(npitch)])
    jump_scale = -STEP_RATE * 0.75 * r_scale / (1.0 - r**total)
    jump_weights = [
        near_first * (jump_scale * (r**i + r ** (i + 1)))
        + near_last * (jump_scale * (r ** (cells - i) + r ** (cells - 1 - i)))
        for i in range(cells)
    ]
    flux_scale = -STEP_RATE * 0.75 * r_scale * (r - 1.0 / r)

    coef_copy.wait()

    def solve_field(f, carry):
        for t in range(tiles):
            at = pl.ds(t * 8, 8)
            jump = None
            for part in range(2):
                for k in range(harm_max):
                    term = waves[part, pl.ds(k, 1), :] * co[part, k, f, at, :]
                    jump = term if jump is None else jump + term
            x = [u[f, i, at, :] for i in range(cells)]
            y = [flux[f, i, at, :] for i in range(cells)]
            back_x, back_y = [None] * cells, [None] * cells
            carry_x, carry_y = q * x[cells - 1], y[cells - 1]
            for i in reversed(range(cells - 1)):
                back_x[i], back_y[i] = carry_x, carry_y
                if i > 0:
                    carry_x = q * (x[i] + carry_x)
                    carry_y = y[i] + r * carry_y
            front_x, front_y = None, None
            for i in range(cells):
                front_x = x[i] if front_x is None else x[i] + q * front_x
                value = out_ref[f, i, at, :] + jump_weights[i] * jump
                relaxed = front_x if back_x[i] is None else front_x + back_x[i]
                value = value + q_scale * relaxed
                slope = front_y
                if back_y[i] is not None:
                    slope = -back_y[i] if slope is None else slope - back_y[i]
                value = value + (flux_scale * r) * slope
                front_y = y[i] if front_y is None else y[i] + r * front_y
                out_ref[f, i, at, :] = value
        return carry

    lax.fori_loop(0, fields, solve_field, 0)

    for copy in sum_copies:
        copy.wait_recv()
    r_wrap = 1.0 / (1.0 - r**total)
    q_wrap = 1.0 / (1.0 - q**total)

    def carry_field(f, carry):
        for t in range(tiles):
            at = pl.ds(t * 8, 8)
            joined = []
            for s, (root, wrap) in enumerate(
                ((r, r_wrap), (r, r_wrap), (q, q_wrap), (q, q_wrap))
            ):
                value = (wrap * root ** (cells * (npitch - 1))) * sums[s, f, at, :]
                for step in range(1, npitch):
                    distance = step - 1 if s % 2 == 0 else npitch - 1 - step
                    factor = wrap * root ** (cells * distance)
                    value = value + factor * got_sums[step - 1, s, f, at, :]
                joined.append(value)
            for i in range(cells):
                out_ref[f, i, at, :] = (
                    out_ref[f, i, at, :]
                    + (flux_scale * r ** (i + 1)) * joined[0]
                    - (flux_scale * r ** (cells - i)) * joined[1]
                    + (q_scale * q ** (i + 1)) * joined[2]
                    + (q_scale * q ** (cells - i)) * joined[3]
                )
        return carry

    lax.fori_loop(0, fields, carry_field, 0)

    when(has_left, right_copy.wait_recv)
    when(has_right, left_copy.wait_recv)
    place = lane % 8
    outer = jnp.logical_or(lane < 4, lane >= 124)

    def span_field(f, carry):
        for g in range(sp_own.shape[1]):
            delta = jnp.where(place < 4, got_left[f, g], got_right[f, g]) - sp_own[f, g]
            ends = jnp.zeros((8, 128), jnp.float32)
            for t in range(4):
                ends = ends + jnp.where(
                    jnp.logical_and(place >= 4, place + t < 8),
                    EDGE[t] * weight,
                    0.0,
                ) * pltpu.roll(delta, 4 - t, 1)
                ends = ends + jnp.where(
                    jnp.logical_and(place < 4, place >= t),
                    EDGE[t] * weight,
                    0.0,
                ) * pltpu.roll(delta, 124 + t, 1)
            for k in range(16):
                i, t = g * half + k // tiles, k % tiles
                moved = pltpu.roll(ends, (124 - 8 * k) % 128, 1)
                out_ref[f, i, t * 8 : t * 8 + 8, :] += jnp.where(outer, moved, 0.0)
        return carry

    lax.fori_loop(0, fields, span_field, 0)

    when(has_up, down_copy.wait_recv)
    when(has_down, up_copy.wait_recv)
    step_row = row % 4

    def axial_field(f, carry):
        for k in range(cells // 2):
            delta = got_tail[f, k] - ax_tail[f, k]
            ends = (EDGE[0] * weight) * delta
            for t in range(1, 4):
                ends = ends + jnp.where(step_row + t < 4, EDGE[t] * weight, 0.0) * pltpu.roll(
                    delta, 8 - t, 0
                )
            out_ref[f, 2 * k, :8, :] += jnp.where(low_rows, ends, 0.0)
            out_ref[f, 2 * k + 1, :8, :] += jnp.where(low_rows, pltpu.roll(ends, 4, 0), 0.0)
            delta = got_head[f, k] - ax_head[f, k]
            ends = (EDGE[0] * weight) * delta
            for t in range(1, 4):
                ends = ends + jnp.where(step_row >= t, EDGE[t] * weight, 0.0) * pltpu.roll(
                    delta, t, 0
                )
            out_ref[f, 2 * k, rows - 8 :, :] += jnp.where(low_rows, 0.0, pltpu.roll(ends, 4, 0))
            out_ref[f, 2 * k + 1, rows - 8 :, :] += jnp.where(low_rows, 0.0, ends)
        return carry

    lax.fori_loop(0, fields, axial_field, 0)

    for copy in sum_copies:
        copy.wait_send()
    when(has_down, down_copy.wait_send)
    when(has_up, up_copy.wait_send)
    when(has_right, right_copy.wait_send)
    when(has_left, left_copy.wait_send)


def shards(sizes, state, coeffs, lag_shift, harmonics):
    fields, cells, rows, lanes = state.shape
    npitch = sizes[0]
    groups = cells * (rows // 8) // 16
    vmem = lambda *shape: pltpu.VMEM(shape, jnp.float32)
    halo = (fields, cells // 2, 8, lanes)
    packed = (fields, groups, 8, lanes)
    sems = 4 + npitch - 1
    return pl.pallas_call(
        functools.partial(kernel, sizes),
        out_shape=jax.ShapeDtypeStruct(state.shape, jnp.float32),
        in_specs=[
            pl.BlockSpec(memory_space=pltpu.SMEM),
            pl.BlockSpec(memory_space=pltpu.VMEM),
            pl.BlockSpec(memory_space=pltpu.HBM),
            pl.BlockSpec(memory_space=pltpu.HBM),
        ],
        out_specs=pl.BlockSpec(memory_space=pltpu.VMEM),
        scratch_shapes=[
            vmem(*state.shape),
            vmem(*coeffs.shape),
            vmem(*state.shape),
            vmem(4, fields, rows, lanes),
            vmem(npitch - 1, 4, fields, rows, lanes),
            vmem(*halo),
            vmem(*halo),
            vmem(*halo),
            vmem(*halo),
            vmem(*packed),
            vmem(*packed),
            vmem(*packed),
            vmem(2, 8, lanes),
            pltpu.SemaphoreType.DMA((2,)),
            pltpu.SemaphoreType.DMA((sems,)),
            pltpu.SemaphoreType.DMA((sems,)),
        ],
        compiler_params=pltpu.CompilerParams(collective_id=0, has_side_effects=True),
    )(lag_shift, harmonics.reshape(1, lanes), state, coeffs)


def solution(mesh):
    sizes = tuple(mesh.shape[name] for name in ("pitch", "axial", "span"))
    placed = (
        P(None, "pitch", "axial", "span"),
        P(None, None, None, "axial", "span"),
        P(),
        P("span"),
    )
    return jax.shard_map(
        functools.partial(shards, sizes),
        mesh=mesh,
        in_specs=placed,
        out_specs=P(None, "pitch", "axial", "span"),
        check_vma=False,
    )
```

```python
import functools
import math

import jax
import jax.numpy as jnp
from jax import lax
from jax.experimental import pallas as pl
from jax.experimental.pallas import tpu as pltpu
from jax.sharding import PartitionSpec as P

PERIOD_SAMPLES = 64
HEAT_RATIO_GAS = 1.4
STEP_RATE = 0.25
DAMPING = 0.5
EDGE = (1.0, -8.0, 28.0, -56.0)
MESH = pl.DeviceIdType.MESH


def line_root(main, side):
    root = (-main + math.sqrt(main * main - 4.0 * side * side)) / (2.0 * side)
    return root, 1.0 / (main + 2.0 * side * root)


def pick(position, values):
    chosen = jnp.float32(values[-1])
    for index in range(len(values) - 1):
        chosen = jnp.where(position == index, jnp.float32(values[index]), chosen)
    return chosen


def kernel(
    sizes,
    lag_ref,
    harm_ref,
    state_hbm,
    coef_hbm,
    out_ref,
    u,
    co,
    flux,
    sums,
    got_sums,
    ax_tail,
    ax_head,
    got_tail,
    got_head,
    sp_own,
    got_left,
    got_right,
    waves,
    local_sem,
    send_sem,
    recv_sem,
):
    npitch, naxial, nspan = sizes
    fields, cells, rows, _ = u.shape
    tiles = rows // 8
    harm_max = co.shape[1]
    total = cells * npitch
    diffusion = float(total * total // 64)
    r, r_scale = line_root(1.0, 0.25)
    q, q_scale = line_root(1.0 + 2.0 * diffusion, -diffusion)
    pitch, axial, span = (lax.axis_index(name) for name in ("pitch", "axial", "span"))

    state_copy = pltpu.make_async_copy(state_hbm, u, local_sem.at[0])
    coef_copy = pltpu.make_async_copy(coef_hbm, co, local_sem.at[1])
    state_copy.start()

    barrier = pltpu.get_barrier_semaphore()

    def greet(**where):
        pl.semaphore_signal(barrier, inc=1, device_id=where, device_id_type=MESH)

    has_up, has_down = axial > 0, axial < naxial - 1
    has_left, has_right = span > 0, span < nspan - 1

    @pl.when(has_up)
    def _():
        greet(axial=axial - 1)

    @pl.when(has_down)
    def _():
        greet(axial=axial + 1)

    @pl.when(has_left)
    def _():
        greet(span=span - 1)

    @pl.when(has_right)
    def _():
        greet(span=span + 1)

    for step in range(1, npitch):
        greet(pitch=lax.rem(pitch + step, npitch))
    coef_copy.start()

    row = lax.broadcasted_iota(jnp.int32, (8, 128), 0)
    lane = lax.broadcasted_iota(jnp.int32, (8, 128), 1)
    group = lane // 8
    low_rows = row < 4

    state_copy.wait()

    def pack_axial(f, carry):
        for k in range(cells // 2):
            a, b = u[f, 2 * k, rows - 8 :, :], u[f, 2 * k + 1, rows - 8 :, :]
            ax_tail[f, k] = jnp.where(low_rows, pltpu.roll(a, 4, 0), b)
            a, b = u[f, 2 * k, :8, :], u[f, 2 * k + 1, :8, :]
            ax_head[f, k] = jnp.where(low_rows, a, pltpu.roll(b, 4, 0))
        return carry

    lax.fori_loop(0, fields, pack_axial, 0)

    neighbours = npitch - 1
    for flag in (has_up, has_down, has_left, has_right):
        neighbours = neighbours + jnp.where(flag, 1, 0)
    pl.semaphore_wait(barrier, neighbours)

    def remote(src, dst, slot, **where):
        return pltpu.make_async_remote_copy(
            src_ref=src,
            dst_ref=dst,
            send_sem=send_sem.at[slot],
            recv_sem=recv_sem.at[slot],
            device_id=where,
            device_id_type=MESH,
        )

    down_copy = remote(ax_tail, got_tail, 0, axial=axial + 1)
    up_copy = remote(ax_head, got_head, 1, axial=axial - 1)
    right_copy = remote(sp_own, got_left, 2, span=span + 1)
    left_copy = remote(sp_own, got_right, 3, span=span - 1)

    def when(flag, action):
        @pl.when(flag)
        def _():
            action()

    def clear(ref):
        ref[...] = jnp.zeros_like(ref)

    when(has_down, down_copy.start)
    when(has_up, up_copy.start)

    half = cells // (sp_own.shape[1])

    def pack_span(f, carry):
        for g in range(sp_own.shape[1]):
            packed = jnp.zeros((8, 128), jnp.float32)
            for k in range(16):
                tile = u[f, g * half + k // tiles, (k % tiles) * 8 : (k % tiles) * 8 + 8, :]
                packed = jnp.where(group == k, pltpu.roll(tile, (8 * k + 4) % 128, 1), packed)
            sp_own[f, g] = packed
        return carry

    lax.fori_loop(0, fields, pack_span, 0)
    when(has_right, right_copy.start)
    when(has_left, left_copy.start)

    def flux_tile(t, carry):
        at = pl.ds(pl.multiple_of(t * 8, 8), 8)
        parts = [None] * 4
        for i in range(cells):
            cell = [u[f, i, at, :] for f in range(fields)]
            inverse = 1.0 / cell[0]
            speed = cell[2] * inverse
            kinetic = 0.5 * (cell[1] * cell[1] + cell[2] * cell[2] + cell[3] * cell[3]) * inverse
            pressure = (HEAT_RATIO_GAS - 1.0) * (cell[4] - kinetic)
            values = [
                cell[2],
                cell[1] * speed,
                cell[2] * speed + pressure,
                cell[3] * speed,
                (cell[4] + pressure) * speed,
            ]
            for f in range(fields):
                flux[f, i, at, :] = values[f]
            if i == 0:
                parts = [list(values), list(values), list(cell), list(cell)]
            else:
                for f in range(fields):
                    parts[0][f] = r * parts[0][f] + values[f]
                    parts[1][f] = parts[1][f] + (r**i) * values[f]
                    parts[2][f] = q * parts[2][f] + cell[f]
                    parts[3][f] = parts[3][f] + (q**i) * cell[f]
        for s in range(4):
            for f in range(fields):
                sums[s, f, at, :] = parts[s][f]
        return carry

    lax.fori_loop(0, tiles, flux_tile, 0)

    sum_copies = [
        remote(sums, got_sums.at[step - 1], 3 + step, pitch=lax.rem(pitch + step, npitch))
        for step in range(1, npitch)
    ]
    for copy in sum_copies:
        copy.start()

    when(jnp.logical_not(has_up), lambda: clear(got_tail))
    when(jnp.logical_not(has_down), lambda: clear(got_head))
    when(jnp.logical_not(has_left), lambda: clear(got_left))
    when(jnp.logical_not(has_right), lambda: clear(got_right))

    weight = -DAMPING / 256.0

    def damp_field(f, carry):
        for i in range(cells):
            x = u[f, i]
            result = (140.0 * weight) * x
            for o, c in ((1, -56.0), (2, 28.0), (3, -8.0), (4, 1.0)):
                pair = (pltpu.roll(x, o, 0) + pltpu.roll(x, rows - o, 0)) + (
                    pltpu.roll(x, o, 1) + pltpu.roll(x, 128 - o, 1)
                )
                result = result + (c * weight) * pair
            out_ref[f, i] = result
        return carry

    lax.fori_loop(0, fields, damp_field, 0)

    order = row.astype(jnp.float32) + 1.0
    phase = (2.0 * math.pi / PERIOD_SAMPLES) * order * lag_ref[0].astype(jnp.float32)
    active = row < harm_ref[...]
    waves[0] = jnp.where(active, jnp.cos(phase), 0.0)
    waves[1] = jnp.where(active, jnp.sin(phase), 0.0)
    near_first = pick(pitch, [r ** (cells * p) for p in range(npitch)])
    near_last = pick(pitch, [r ** (cells * (npitch - 1 - p)) for p in range(npitch)])
    jump_scale = -STEP_RATE * 0.75 * r_scale / (1.0 - r**total)
    jump_weights = [
        near_first * (jump_scale * (r**i + r ** (i + 1)))
        + near_last * (jump_scale * (r ** (cells - i) + r ** (cells - 1 - i)))
        for i in range(cells)
    ]
    flux_scale = -STEP_RATE * 0.75 * r_scale * (r - 1.0 / r)

    coef_copy.wait()

    def solve_field(f, carry):
        for t in range(tiles):
            at = pl.ds(t * 8, 8)
            jump = None
            for part in range(2):
                for k in range(harm_max):
                    term = waves[part, pl.ds(k, 1), :] * co[part, k, f, at, :]
                    jump = term if jump is None else jump + term
            x = [u[f, i, at, :] for i in range(cells)]
            y = [flux[f, i, at, :] for i in range(cells)]
            back_x, back_y = [None] * cells, [None] * cells
            carry_x, carry_y = q * x[cells - 1], y[cells - 1]
            for i in reversed(range(cells - 1)):
                back_x[i], back_y[i] = carry_x, carry_y
                if i > 0:
                    carry_x = q * (x[i] + carry_x)
                    carry_y = y[i] + r * carry_y
            front_x, front_y = None, None
            for i in range(cells):
                front_x = x[i] if front_x is None else x[i] + q * front_x
                value = out_ref[f, i, at, :] + jump_weights[i] * jump
                relaxed = front_x if back_x[i] is None else front_x + back_x[i]
                value = value + q_scale * relaxed
                slope = front_y
                if back_y[i] is not None:
                    slope = -back_y[i] if slope is None else slope - back_y[i]
                value = value + (flux_scale * r) * slope
                front_y = y[i] if front_y is None else y[i] + r * front_y
                out_ref[f, i, at, :] = value
        return carry

    lax.fori_loop(0, fields, solve_field, 0)

    for copy in sum_copies:
        copy.wait_recv()
    r_wrap = 1.0 / (1.0 - r**total)
    q_wrap = 1.0 / (1.0 - q**total)

    def carry_field(f, carry):
        for t in range(tiles):
            at = pl.ds(t * 8, 8)
            joined = []
            for s, (root, wrap) in enumerate(
                ((r, r_wrap), (r, r_wrap), (q, q_wrap), (q, q_wrap))
            ):
                value = (wrap * root ** (cells * (npitch - 1))) * sums[s, f, at, :]
                for step in range(1, npitch):
                    distance = step - 1 if s % 2 == 0 else npitch - 1 - step
                    factor = wrap * root ** (cells * distance)
                    value = value + factor * got_sums[step - 1, s, f, at, :]
                joined.append(value)
            for i in range(cells):
                out_ref[f, i, at, :] = (
                    out_ref[f, i, at, :]
                    + (flux_scale * r ** (i + 1)) * joined[0]
                    - (flux_scale * r ** (cells - i)) * joined[1]
                    + (q_scale * q ** (i + 1)) * joined[2]
                    + (q_scale * q ** (cells - i)) * joined[3]
                )
        return carry

    lax.fori_loop(0, fields, carry_field, 0)

    when(has_left, right_copy.wait_recv)
    when(has_right, left_copy.wait_recv)
    place = lane % 8
    outer = jnp.logical_or(lane < 4, lane >= 124)

    def span_field(f, carry):
        for g in range(sp_own.shape[1]):
            delta = jnp.where(place < 4, got_left[f, g], got_right[f, g]) - sp_own[f, g]
            ends = jnp.zeros((8, 128), jnp.float32)
            for t in range(4):
                ends = ends + jnp.where(
                    jnp.logical_and(place >= 4, place + t < 8),
                    EDGE[t] * weight,
                    0.0,
                ) * pltpu.roll(delta, 4 - t, 1)
                ends = ends + jnp.where(
                    jnp.logical_and(place < 4, place >= t),
                    EDGE[t] * weight,
                    0.0,
                ) * pltpu.roll(delta, 124 + t, 1)
            for k in range(16):
                i, t = g * half + k // tiles, k % tiles
                moved = pltpu.roll(ends, (124 - 8 * k) % 128, 1)
                out_ref[f, i, t * 8 : t * 8 + 8, :] += jnp.where(outer, moved, 0.0)
        return carry

    lax.fori_loop(0, fields, span_field, 0)

    when(has_up, down_copy.wait_recv)
    when(has_down, up_copy.wait_recv)
    step_row = row % 4

    def axial_field(f, carry):
        for k in range(cells // 2):
            delta = got_tail[f, k] - ax_tail[f, k]
            ends = (EDGE[0] * weight) * delta
            for t in range(1, 4):
                ends = ends + jnp.where(step_row + t < 4, EDGE[t] * weight, 0.0) * pltpu.roll(
                    delta, 8 - t, 0
                )
            out_ref[f, 2 * k, :8, :] += jnp.where(low_rows, ends, 0.0)
            out_ref[f, 2 * k + 1, :8, :] += jnp.where(low_rows, pltpu.roll(ends, 4, 0), 0.0)
            delta = got_head[f, k] - ax_head[f, k]
            ends = (EDGE[0] * weight) * delta
            for t in range(1, 4):
                ends = ends + jnp.where(step_row >= t, EDGE[t] * weight, 0.0) * pltpu.roll(
                    delta, t, 0
                )
            out_ref[f, 2 * k, rows - 8 :, :] += jnp.where(low_rows, 0.0, pltpu.roll(ends, 4, 0))
            out_ref[f, 2 * k + 1, rows - 8 :, :] += jnp.where(low_rows, 0.0, ends)
        return carry

    lax.fori_loop(0, fields, axial_field, 0)

    for copy in sum_copies:
        copy.wait_send()
    when(has_down, down_copy.wait_send)
    when(has_up, up_copy.wait_send)
    when(has_right, right_copy.wait_send)
    when(has_left, left_copy.wait_send)


def shards(sizes, state, coeffs, lag_shift, harmonics):
    fields, cells, rows, lanes = state.shape
    npitch = sizes[0]
    groups = cells * (rows // 8) // 16
    vmem = lambda *shape: pltpu.VMEM(shape, jnp.float32)
    halo = (fields, cells // 2, 8, lanes)
    packed = (fields, groups, 8, lanes)
    sems = 4 + npitch - 1
    return pl.pallas_call(
        functools.partial(kernel, sizes),
        out_shape=pltpu.VMEM(state.shape, jnp.float32),
        in_specs=[
            pl.BlockSpec(memory_space=pltpu.SMEM),
            pl.BlockSpec(memory_space=pltpu.VMEM),
            pl.BlockSpec(memory_space=pltpu.HBM),
            pl.BlockSpec(memory_space=pltpu.HBM),
        ],
        out_specs=pl.BlockSpec(memory_space=pltpu.VMEM),
        scratch_shapes=[
            vmem(*state.shape),
            vmem(*coeffs.shape),
            vmem(*state.shape),
            vmem(4, fields, rows, lanes),
            vmem(npitch - 1, 4, fields, rows, lanes),
            vmem(*halo),
            vmem(*halo),
            vmem(*halo),
            vmem(*halo),
            vmem(*packed),
            vmem(*packed),
            vmem(*packed),
            vmem(2, 8, lanes),
            pltpu.SemaphoreType.DMA((2,)),
            pltpu.SemaphoreType.DMA((sems,)),
            pltpu.SemaphoreType.DMA((sems,)),
        ],
        compiler_params=pltpu.CompilerParams(collective_id=0, has_side_effects=True),
    )(lag_shift, harmonics.reshape(1, lanes), state, coeffs)


def solution(mesh):
    sizes = tuple(mesh.shape[name] for name in ("pitch", "axial", "span"))
    placed = (
        P(None, "pitch", "axial", "span"),
        P(None, None, None, "axial", "span"),
        P(),
        P("span"),
    )
    return jax.shard_map(
        functools.partial(shards, sizes),
        mesh=mesh,
        in_specs=placed,
        out_specs=P(None, "pitch", "axial", "span"),
        check_vma=False,
    )
```

```python
import functools
import math

import jax
import jax.numpy as jnp
from jax import lax
from jax.experimental import pallas as pl
from jax.experimental.pallas import tpu as pltpu
from jax.sharding import PartitionSpec as P

PERIOD_SAMPLES = 64
HEAT_RATIO_GAS = 1.4
STEP_RATE = 0.25
DAMPING = 0.5
EDGE = (1.0, -8.0, 28.0, -56.0)
MESH = pl.DeviceIdType.MESH


def line_root(main, side):
    root = (-main + math.sqrt(main * main - 4.0 * side * side)) / (2.0 * side)
    return root, 1.0 / (main + 2.0 * side * root)


def pick(position, values):
    chosen = jnp.float32(values[-1])
    for index in range(len(values) - 1):
        chosen = jnp.where(position == index, jnp.float32(values[index]), chosen)
    return chosen


def kernel(
    sizes,
    lag_hbm,
    harm_hbm,
    state_hbm,
    coef_hbm,
    out_ref,
    u,
    co,
    flux,
    sums,
    got_sums,
    ax_tail,
    ax_head,
    got_tail,
    got_head,
    sp_own,
    got_left,
    got_right,
    waves,
    lag_ref,
    harm_ref,
    local_sem,
    send_sem,
    recv_sem,
):
    npitch, naxial, nspan = sizes
    fields, cells, rows, _ = u.shape
    tiles = rows // 8
    harm_max = co.shape[1]
    total = cells * npitch
    diffusion = float(total * total // 64)
    r, r_scale = line_root(1.0, 0.25)
    q, q_scale = line_root(1.0 + 2.0 * diffusion, -diffusion)
    pitch, axial, span = (lax.axis_index(name) for name in ("pitch", "axial", "span"))

    state_copy = pltpu.make_async_copy(state_hbm, u, local_sem.at[0])
    coef_copy = pltpu.make_async_copy(coef_hbm, co, local_sem.at[1])
    state_copy.start()

    barrier = pltpu.get_barrier_semaphore()

    def greet(**where):
        pl.semaphore_signal(barrier, inc=1, device_id=where, device_id_type=MESH)

    has_up, has_down = axial > 0, axial < naxial - 1
    has_left, has_right = span > 0, span < nspan - 1

    @pl.when(has_up)
    def _():
        greet(axial=axial - 1)

    @pl.when(has_down)
    def _():
        greet(axial=axial + 1)

    @pl.when(has_left)
    def _():
        greet(span=span - 1)

    @pl.when(has_right)
    def _():
        greet(span=span + 1)

    for step in range(1, npitch):
        greet(pitch=lax.rem(pitch + step, npitch))
    coef_copy.start()
    small_copies = [
        pltpu.make_async_copy(lag_hbm, lag_ref, local_sem.at[2]),
        pltpu.make_async_copy(harm_hbm, harm_ref, local_sem.at[3]),
    ]
    for copy in small_copies:
        copy.start()

    row = lax.broadcasted_iota(jnp.int32, (8, 128), 0)
    lane = lax.broadcasted_iota(jnp.int32, (8, 128), 1)
    group = lane // 8
    low_rows = row < 4

    state_copy.wait()

    def pack_axial(f, carry):
        for k in range(cells // 2):
            a, b = u[f, 2 * k, rows - 8 :, :], u[f, 2 * k + 1, rows - 8 :, :]
            ax_tail[f, k] = jnp.where(low_rows, pltpu.roll(a, 4, 0), b)
            a, b = u[f, 2 * k, :8, :], u[f, 2 * k + 1, :8, :]
            ax_head[f, k] = jnp.where(low_rows, a, pltpu.roll(b, 4, 0))
        return carry

    lax.fori_loop(0, fields, pack_axial, 0, unroll=True)

    neighbours = npitch - 1
    for flag in (has_up, has_down, has_left, has_right):
        neighbours = neighbours + jnp.where(flag, 1, 0)
    pl.semaphore_wait(barrier, neighbours)

    def remote(src, dst, slot, **where):
        return pltpu.make_async_remote_copy(
            src_ref=src,
            dst_ref=dst,
            send_sem=send_sem.at[slot],
            recv_sem=recv_sem.at[slot],
            device_id=where,
            device_id_type=MESH,
        )

    down_copy = remote(ax_tail, got_tail, 0, axial=axial + 1)
    up_copy = remote(ax_head, got_head, 1, axial=axial - 1)
    right_copy = remote(sp_own, got_left, 2, span=span + 1)
    left_copy = remote(sp_own, got_right, 3, span=span - 1)

    def when(flag, action):
        @pl.when(flag)
        def _():
            action()

    def clear(ref):
        ref[...] = jnp.zeros_like(ref)

    odd = lax.rem(axial, 2) == 1
    when(jnp.logical_and(has_up, odd), up_copy.start)
    when(has_down, down_copy.start)
    when(jnp.logical_and(has_up, jnp.logical_not(odd)), up_copy.start)

    half = cells // (sp_own.shape[1])

    def pack_span(f, carry):
        for g in range(sp_own.shape[1]):
            packed = jnp.zeros((8, 128), jnp.float32)
            for k in range(16):
                tile = u[f, g * half + k // tiles, (k % tiles) * 8 : (k % tiles) * 8 + 8, :]
                packed = jnp.where(group == k, pltpu.roll(tile, (8 * k + 4) % 128, 1), packed)
            sp_own[f, g] = packed
        return carry

    lax.fori_loop(0, fields, pack_span, 0, unroll=True)
    when(has_right, right_copy.start)
    when(has_left, left_copy.start)

    def flux_tile(t, carry):
        at = pl.ds(pl.multiple_of(t * 8, 8), 8)
        parts = [None] * 4
        for i in range(cells):
            cell = [u[f, i, at, :] for f in range(fields)]
            inverse = 1.0 / cell[0]
            speed = cell[2] * inverse
            kinetic = 0.5 * (cell[1] * cell[1] + cell[2] * cell[2] + cell[3] * cell[3]) * inverse
            pressure = (HEAT_RATIO_GAS - 1.0) * (cell[4] - kinetic)
            values = [
                cell[2],
                cell[1] * speed,
                cell[2] * speed + pressure,
                cell[3] * speed,
                (cell[4] + pressure) * speed,
            ]
            for f in range(fields):
                flux[f, i, at, :] = values[f]
            if i == 0:
                parts = [list(values), list(values), list(cell), list(cell)]
            else:
                for f in range(fields):
                    parts[0][f] = r * parts[0][f] + values[f]
                    parts[1][f] = parts[1][f] + (r**i) * values[f]
                    parts[2][f] = q * parts[2][f] + cell[f]
                    parts[3][f] = parts[3][f] + (q**i) * cell[f]
        for s in range(4):
            for f in range(fields):
                sums[s, f, at, :] = parts[s][f]
        return carry

    lax.fori_loop(0, tiles, flux_tile, 0, unroll=True)

    sum_copies = [
        remote(sums, got_sums.at[step - 1], 3 + step, pitch=lax.rem(pitch + step, npitch))
        for step in range(1, npitch)
    ]
    for copy in sum_copies:
        copy.start()

    when(jnp.logical_not(has_up), lambda: clear(got_tail))
    when(jnp.logical_not(has_down), lambda: clear(got_head))
    when(jnp.logical_not(has_left), lambda: clear(got_left))
    when(jnp.logical_not(has_right), lambda: clear(got_right))

    weight = -DAMPING / 256.0

    def damp_field(f, carry):
        for i in range(cells):
            x = u[f, i]
            result = (140.0 * weight) * x
            for o, c in ((1, -56.0), (2, 28.0), (3, -8.0), (4, 1.0)):
                pair = (pltpu.roll(x, o, 0) + pltpu.roll(x, rows - o, 0)) + (
                    pltpu.roll(x, o, 1) + pltpu.roll(x, 128 - o, 1)
                )
                result = result + (c * weight) * pair
            out_ref[f, i] = result
        return carry

    lax.fori_loop(0, fields, damp_field, 0, unroll=True)

    for copy in small_copies:
        copy.wait()
    order = row.astype(jnp.float32) + 1.0
    phase = (2.0 * math.pi / PERIOD_SAMPLES) * order * lag_ref[0].astype(jnp.float32)
    active = row < harm_ref[...]
    waves[0] = jnp.where(active, jnp.cos(phase), 0.0)
    waves[1] = jnp.where(active, jnp.sin(phase), 0.0)
    near_first = pick(pitch, [r ** (cells * p) for p in range(npitch)])
    near_last = pick(pitch, [r ** (cells * (npitch - 1 - p)) for p in range(npitch)])
    jump_scale = -STEP_RATE * 0.75 * r_scale / (1.0 - r**total)
    jump_weights = [
        near_first * (jump_scale * (r**i + r ** (i + 1)))
        + near_last * (jump_scale * (r ** (cells - i) + r ** (cells - 1 - i)))
        for i in range(cells)
    ]
    flux_scale = -STEP_RATE * 0.75 * r_scale * (r - 1.0 / r)

    coef_copy.wait()

    def solve_field(f, carry):
        for t in range(tiles):
            at = pl.ds(t * 8, 8)
            jump = None
            for part in range(2):
                for k in range(harm_max):
                    term = waves[part, pl.ds(k, 1), :] * co[part, k, f, at, :]
                    jump = term if jump is None else jump + term
            x = [u[f, i, at, :] for i in range(cells)]
            y = [flux[f, i, at, :] for i in range(cells)]
            back_x, back_y = [None] * cells, [None] * cells
            carry_x, carry_y = q * x[cells - 1], y[cells - 1]
            for i in reversed(range(cells - 1)):
                back_x[i], back_y[i] = carry_x, carry_y
                if i > 0:
                    carry_x = q * (x[i] + carry_x)
                    carry_y = y[i] + r * carry_y
            front_x, front_y = None, None
            for i in range(cells):
                front_x = x[i] if front_x is None else x[i] + q * front_x
                value = out_ref[f, i, at, :] + jump_weights[i] * jump
                relaxed = front_x if back_x[i] is None else front_x + back_x[i]
                value = value + q_scale * relaxed
                slope = front_y
                if back_y[i] is not None:
                    slope = -back_y[i] if slope is None else slope - back_y[i]
                value = value + (flux_scale * r) * slope
                front_y = y[i] if front_y is None else y[i] + r * front_y
                out_ref[f, i, at, :] = value
        return carry

    lax.fori_loop(0, fields, solve_field, 0, unroll=True)

    for copy in sum_copies:
        copy.wait_recv()
    r_wrap = 1.0 / (1.0 - r**total)
    q_wrap = 1.0 / (1.0 - q**total)

    def carry_field(f, carry):
        for t in range(tiles):
            at = pl.ds(t * 8, 8)
            joined = []
            for s, (root, wrap) in enumerate(
                ((r, r_wrap), (r, r_wrap), (q, q_wrap), (q, q_wrap))
            ):
                value = (wrap * root ** (cells * (npitch - 1))) * sums[s, f, at, :]
                for step in range(1, npitch):
                    distance = step - 1 if s % 2 == 0 else npitch - 1 - step
                    factor = wrap * root ** (cells * distance)
                    value = value + factor * got_sums[step - 1, s, f, at, :]
                joined.append(value)
            for i in range(cells):
                out_ref[f, i, at, :] = (
                    out_ref[f, i, at, :]
                    + (flux_scale * r ** (i + 1)) * joined[0]
                    - (flux_scale * r ** (cells - i)) * joined[1]
                    + (q_scale * q ** (i + 1)) * joined[2]
                    + (q_scale * q ** (cells - i)) * joined[3]
                )
        return carry

    lax.fori_loop(0, fields, carry_field, 0, unroll=True)

    when(has_left, right_copy.wait_recv)
    when(has_right, left_copy.wait_recv)
    place = lane % 8
    outer = jnp.logical_or(lane < 4, lane >= 124)

    def span_field(f, carry):
        for g in range(sp_own.shape[1]):
            delta = jnp.where(place < 4, got_left[f, g], got_right[f, g]) - sp_own[f, g]
            ends = jnp.zeros((8, 128), jnp.float32)
            for t in range(4):
                ends = ends + jnp.where(
                    jnp.logical_and(place >= 4, place + t < 8),
                    EDGE[t] * weight,
                    0.0,
                ) * pltpu.roll(delta, 4 - t, 1)
                ends = ends + jnp.where(
                    jnp.logical_and(place < 4, place >= t),
                    EDGE[t] * weight,
                    0.0,
                ) * pltpu.roll(delta, 124 + t, 1)
            for k in range(16):
                i, t = g * half + k // tiles, k % tiles
                moved = pltpu.roll(ends, (124 - 8 * k) % 128, 1)
                out_ref[f, i, t * 8 : t * 8 + 8, :] += jnp.where(outer, moved, 0.0)
        return carry

    lax.fori_loop(0, fields, span_field, 0, unroll=True)

    when(has_up, down_copy.wait_recv)
    when(has_down, up_copy.wait_recv)
    step_row = row % 4

    def axial_field(f, carry):
        for k in range(cells // 2):
            delta = got_tail[f, k] - ax_tail[f, k]
            ends = (EDGE[0] * weight) * delta
            for t in range(1, 4):
                ends = ends + jnp.where(step_row + t < 4, EDGE[t] * weight, 0.0) * pltpu.roll(
                    delta, 8 - t, 0
                )
            out_ref[f, 2 * k, :8, :] += jnp.where(low_rows, ends, 0.0)
            out_ref[f, 2 * k + 1, :8, :] += jnp.where(low_rows, pltpu.roll(ends, 4, 0), 0.0)
            delta = got_head[f, k] - ax_head[f, k]
            ends = (EDGE[0] * weight) * delta
            for t in range(1, 4):
                ends = ends + jnp.where(step_row >= t, EDGE[t] * weight, 0.0) * pltpu.roll(
                    delta, t, 0
                )
            out_ref[f, 2 * k, rows - 8 :, :] += jnp.where(low_rows, 0.0, pltpu.roll(ends, 4, 0))
            out_ref[f, 2 * k + 1, rows - 8 :, :] += jnp.where(low_rows, 0.0, ends)
        return carry

    lax.fori_loop(0, fields, axial_field, 0, unroll=True)

    for copy in sum_copies:
        copy.wait_send()
    when(has_down, down_copy.wait_send)
    when(has_up, up_copy.wait_send)
    when(has_right, right_copy.wait_send)
    when(has_left, left_copy.wait_send)


def shards(sizes, state, coeffs, lag_shift, harmonics):
    fields, cells, rows, lanes = state.shape
    npitch = sizes[0]
    groups = cells * (rows // 8) // 16
    vmem = lambda *shape: pltpu.VMEM(shape, jnp.float32)
    halo = (fields, cells // 2, 8, lanes)
    packed = (fields, groups, 8, lanes)
    sems = 4 + npitch - 1
    return pl.pallas_call(
        functools.partial(kernel, sizes),
        out_shape=pltpu.VMEM(state.shape, jnp.float32),
        in_specs=[
            pl.BlockSpec(memory_space=pltpu.HBM),
            pl.BlockSpec(memory_space=pltpu.HBM),
            pl.BlockSpec(memory_space=pltpu.HBM),
            pl.BlockSpec(memory_space=pltpu.HBM),
        ],
        out_specs=pl.BlockSpec(memory_space=pltpu.VMEM),
        scratch_shapes=[
            vmem(*state.shape),
            vmem(*coeffs.shape),
            vmem(*state.shape),
            vmem(4, fields, rows, lanes),
            vmem(npitch - 1, 4, fields, rows, lanes),
            vmem(*halo),
            vmem(*halo),
            vmem(*halo),
            vmem(*halo),
            vmem(*packed),
            vmem(*packed),
            vmem(*packed),
            vmem(2, 8, lanes),
            pltpu.SMEM((1,), jnp.int32),
            pltpu.VMEM((1, lanes), jnp.int32),
            pltpu.SemaphoreType.DMA((4,)),
            pltpu.SemaphoreType.DMA((sems,)),
            pltpu.SemaphoreType.DMA((sems,)),
        ],
        compiler_params=pltpu.CompilerParams(collective_id=0, has_side_effects=True),
    )(lag_shift, harmonics.reshape(1, lanes), state, coeffs)


def solution(mesh):
    sizes = tuple(mesh.shape[name] for name in ("pitch", "axial", "span"))
    placed = (
        P(None, "pitch", "axial", "span"),
        P(None, None, None, "axial", "span"),
        P(),
        P("span"),
    )
    return jax.shard_map(
        functools.partial(shards, sizes),
        mesh=mesh,
        in_specs=placed,
        out_specs=P(None, "pitch", "axial", "span"),
        check_vma=False,
    )
```

```python
import functools
import math

import jax
import jax.numpy as jnp
from jax import lax
from jax.experimental import pallas as pl
from jax.experimental.pallas import tpu as pltpu
from jax.sharding import PartitionSpec as P

PERIOD_SAMPLES = 64
HEAT_RATIO_GAS = 1.4
STEP_RATE = 0.25
DAMPING = 0.5
EDGE = (1.0, -8.0, 28.0, -56.0)
MESH = pl.DeviceIdType.MESH


def line_root(main, side):
    root = (-main + math.sqrt(main * main - 4.0 * side * side)) / (2.0 * side)
    return root, 1.0 / (main + 2.0 * side * root)


def pick(position, values):
    chosen = jnp.float32(values[-1])
    for index in range(len(values) - 1):
        chosen = jnp.where(position == index, jnp.float32(values[index]), chosen)
    return chosen


def kernel(
    sizes,
    lag_hbm,
    harm_hbm,
    state_hbm,
    coef_hbm,
    out_ref,
    u,
    co,
    flux,
    sums,
    got_sums,
    ax_tail,
    ax_head,
    got_tail,
    got_head,
    sp_own,
    got_left,
    got_right,
    waves,
    band,
    lag_ref,
    harm_ref,
    local_sem,
    send_sem,
    recv_sem,
):
    npitch, naxial, nspan = sizes
    fields, cells, rows, _ = u.shape
    tiles = rows // 8
    harm_max = co.shape[1]
    total = cells * npitch
    diffusion = float(total * total // 64)
    r, r_scale = line_root(1.0, 0.25)
    q, q_scale = line_root(1.0 + 2.0 * diffusion, -diffusion)
    pitch, axial, span = (lax.axis_index(name) for name in ("pitch", "axial", "span"))

    state_copy = pltpu.make_async_copy(state_hbm, u, local_sem.at[0])
    coef_copy = pltpu.make_async_copy(coef_hbm, co, local_sem.at[1])
    state_copy.start()

    barrier = pltpu.get_barrier_semaphore()

    def greet(**where):
        pl.semaphore_signal(barrier, inc=1, device_id=where, device_id_type=MESH)

    has_up, has_down = axial > 0, axial < naxial - 1
    has_left, has_right = span > 0, span < nspan - 1

    @pl.when(has_up)
    def _():
        greet(axial=axial - 1)

    @pl.when(has_down)
    def _():
        greet(axial=axial + 1)

    @pl.when(has_left)
    def _():
        greet(span=span - 1)

    @pl.when(has_right)
    def _():
        greet(span=span + 1)

    for step in range(1, npitch):
        greet(pitch=lax.rem(pitch + step, npitch))
    coef_copy.start()
    small_copies = [
        pltpu.make_async_copy(lag_hbm, lag_ref, local_sem.at[2]),
        pltpu.make_async_copy(harm_hbm, harm_ref, local_sem.at[3]),
    ]
    for copy in small_copies:
        copy.start()

    row = lax.broadcasted_iota(jnp.int32, (8, 128), 0)
    lane = lax.broadcasted_iota(jnp.int32, (8, 128), 1)
    group = lane // 8
    low_rows = row < 4

    weight = -DAMPING / 256.0
    gap = (
        lax.broadcasted_iota(jnp.int32, (256, 128), 0)
        - lax.broadcasted_iota(jnp.int32, (256, 128), 1)
        + 256
    ) % 128
    gap = jnp.minimum(gap, 128 - gap)
    taps = jnp.zeros((256, 128), jnp.float32)
    for o, c in enumerate((70.0, -56.0, 28.0, -8.0, 1.0)):
        taps = jnp.where(gap == o, c * weight, taps)
    band[...] = taps.astype(jnp.bfloat16)

    state_copy.wait()

    def pack_axial(f, carry):
        for k in range(cells // 2):
            a, b = u[f, 2 * k, rows - 8 :, :], u[f, 2 * k + 1, rows - 8 :, :]
            ax_tail[f, k] = jnp.where(low_rows, pltpu.roll(a, 4, 0), b)
            a, b = u[f, 2 * k, :8, :], u[f, 2 * k + 1, :8, :]
            ax_head[f, k] = jnp.where(low_rows, a, pltpu.roll(b, 4, 0))
        return carry

    lax.fori_loop(0, fields, pack_axial, 0, unroll=True)

    neighbours = npitch - 1
    for flag in (has_up, has_down, has_left, has_right):
        neighbours = neighbours + jnp.where(flag, 1, 0)
    pl.semaphore_wait(barrier, neighbours)

    def remote(src, dst, slot, **where):
        return pltpu.make_async_remote_copy(
            src_ref=src,
            dst_ref=dst,
            send_sem=send_sem.at[slot],
            recv_sem=recv_sem.at[slot],
            device_id=where,
            device_id_type=MESH,
        )

    down_copy = remote(ax_tail, got_tail, 0, axial=axial + 1)
    up_copy = remote(ax_head, got_head, 1, axial=axial - 1)
    right_copy = remote(sp_own, got_left, 2, span=span + 1)
    left_copy = remote(sp_own, got_right, 3, span=span - 1)

    def when(flag, action):
        @pl.when(flag)
        def _():
            action()

    def clear(ref):
        ref[...] = jnp.zeros_like(ref)

    odd = lax.rem(axial, 2) == 1
    when(jnp.logical_and(has_up, odd), up_copy.start)
    when(has_down, down_copy.start)
    when(jnp.logical_and(has_up, jnp.logical_not(odd)), up_copy.start)

    half = cells // (sp_own.shape[1])

    def pack_span(f, carry):
        for g in range(sp_own.shape[1]):
            packed = jnp.zeros((8, 128), jnp.float32)
            for k in range(16):
                tile = u[f, g * half + k // tiles, (k % tiles) * 8 : (k % tiles) * 8 + 8, :]
                packed = jnp.where(group == k, pltpu.roll(tile, (8 * k + 4) % 128, 1), packed)
            sp_own[f, g] = packed
        return carry

    lax.fori_loop(0, fields, pack_span, 0, unroll=True)
    when(has_right, right_copy.start)
    when(has_left, left_copy.start)

    def flux_tile(t, carry):
        at = pl.ds(pl.multiple_of(t * 8, 8), 8)
        parts = [None] * 4
        for i in range(cells):
            cell = [u[f, i, at, :] for f in range(fields)]
            inverse = 1.0 / cell[0]
            speed = cell[2] * inverse
            kinetic = 0.5 * (cell[1] * cell[1] + cell[2] * cell[2] + cell[3] * cell[3]) * inverse
            pressure = (HEAT_RATIO_GAS - 1.0) * (cell[4] - kinetic)
            values = [
                cell[2],
                cell[1] * speed,
                cell[2] * speed + pressure,
                cell[3] * speed,
                (cell[4] + pressure) * speed,
            ]
            for f in range(fields):
                flux[f, i, at, :] = values[f]
            if i == 0:
                parts = [list(values), list(values), list(cell), list(cell)]
            else:
                for f in range(fields):
                    parts[0][f] = r * parts[0][f] + values[f]
                    parts[1][f] = parts[1][f] + (r**i) * values[f]
                    parts[2][f] = q * parts[2][f] + cell[f]
                    parts[3][f] = parts[3][f] + (q**i) * cell[f]
        for s in range(4):
            for f in range(fields):
                sums[s, f, at, :] = parts[s][f]
        return carry

    lax.fori_loop(0, tiles, flux_tile, 0, unroll=True)

    sum_copies = [
        remote(sums, got_sums.at[step - 1], 3 + step, pitch=lax.rem(pitch + step, npitch))
        for step in range(1, npitch)
    ]
    for copy in sum_copies:
        copy.start()

    when(jnp.logical_not(has_up), lambda: clear(got_tail))
    when(jnp.logical_not(has_down), lambda: clear(got_head))
    when(jnp.logical_not(has_left), lambda: clear(got_left))
    when(jnp.logical_not(has_right), lambda: clear(got_right))


    def damp_field(f, carry):
        block = u[f].reshape(cells * rows, 128)
        high = block.astype(jnp.bfloat16)
        low = (block - high.astype(jnp.float32)).astype(jnp.bfloat16)
        across = jnp.dot(
            jnp.concatenate([high, low], axis=1), band[...], preferred_element_type=jnp.float32
        )
        for i in range(cells):
            x = u[f, i]
            result = across[i * rows : (i + 1) * rows] + (70.0 * weight) * x
            for o, c in ((1, -56.0), (2, 28.0), (3, -8.0), (4, 1.0)):
                pair = pltpu.roll(x, o, 0) + pltpu.roll(x, rows - o, 0)
                result = result + (c * weight) * pair
            out_ref[f, i] = result
        return carry

    lax.fori_loop(0, fields, damp_field, 0, unroll=True)

    for copy in small_copies:
        copy.wait()
    order = row.astype(jnp.float32) + 1.0
    phase = (2.0 * math.pi / PERIOD_SAMPLES) * order * lag_ref[0].astype(jnp.float32)
    active = row < harm_ref[...]
    waves[0] = jnp.where(active, jnp.cos(phase), 0.0)
    waves[1] = jnp.where(active, jnp.sin(phase), 0.0)
    near_first = pick(pitch, [r ** (cells * p) for p in range(npitch)])
    near_last = pick(pitch, [r ** (cells * (npitch - 1 - p)) for p in range(npitch)])
    jump_scale = -STEP_RATE * 0.75 * r_scale / (1.0 - r**total)
    jump_weights = [
        near_first * (jump_scale * (r**i + r ** (i + 1)))
        + near_last * (jump_scale * (r ** (cells - i) + r ** (cells - 1 - i)))
        for i in range(cells)
    ]
    flux_scale = -STEP_RATE * 0.75 * r_scale * (r - 1.0 / r)

    coef_copy.wait()

    def solve_field(f, carry):
        for t in range(tiles):
            at = pl.ds(t * 8, 8)
            jump = None
            for part in range(2):
                for k in range(harm_max):
                    term = waves[part, pl.ds(k, 1), :] * co[part, k, f, at, :]
                    jump = term if jump is None else jump + term
            x = [u[f, i, at, :] for i in range(cells)]
            y = [flux[f, i, at, :] for i in range(cells)]
            back_x, back_y = [None] * cells, [None] * cells
            carry_x, carry_y = q * x[cells - 1], y[cells - 1]
            for i in reversed(range(cells - 1)):
                back_x[i], back_y[i] = carry_x, carry_y
                if i > 0:
                    carry_x = q * (x[i] + carry_x)
                    carry_y = y[i] + r * carry_y
            front_x, front_y = None, None
            for i in range(cells):
                front_x = x[i] if front_x is None else x[i] + q * front_x
                value = out_ref[f, i, at, :] + jump_weights[i] * jump
                relaxed = front_x if back_x[i] is None else front_x + back_x[i]
                value = value + q_scale * relaxed
                slope = front_y
                if back_y[i] is not None:
                    slope = -back_y[i] if slope is None else slope - back_y[i]
                value = value + (flux_scale * r) * slope
                front_y = y[i] if front_y is None else y[i] + r * front_y
                out_ref[f, i, at, :] = value
        return carry

    lax.fori_loop(0, fields, solve_field, 0, unroll=True)

    for copy in sum_copies:
        copy.wait_recv()
    r_wrap = 1.0 / (1.0 - r**total)
    q_wrap = 1.0 / (1.0 - q**total)

    def carry_field(f, carry):
        for t in range(tiles):
            at = pl.ds(t * 8, 8)
            joined = []
            for s, (root, wrap) in enumerate(
                ((r, r_wrap), (r, r_wrap), (q, q_wrap), (q, q_wrap))
            ):
                value = (wrap * root ** (cells * (npitch - 1))) * sums[s, f, at, :]
                for step in range(1, npitch):
                    distance = step - 1 if s % 2 == 0 else npitch - 1 - step
                    factor = wrap * root ** (cells * distance)
                    value = value + factor * got_sums[step - 1, s, f, at, :]
                joined.append(value)
            for i in range(cells):
                out_ref[f, i, at, :] = (
                    out_ref[f, i, at, :]
                    + (flux_scale * r ** (i + 1)) * joined[0]
                    - (flux_scale * r ** (cells - i)) * joined[1]
                    + (q_scale * q ** (i + 1)) * joined[2]
                    + (q_scale * q ** (cells - i)) * joined[3]
                )
        return carry

    lax.fori_loop(0, fields, carry_field, 0, unroll=True)

    when(has_left, right_copy.wait_recv)
    when(has_right, left_copy.wait_recv)
    place = lane % 8
    outer = jnp.logical_or(lane < 4, lane >= 124)

    def span_field(f, carry):
        for g in range(sp_own.shape[1]):
            delta = jnp.where(place < 4, got_left[f, g], got_right[f, g]) - sp_own[f, g]
            ends = jnp.zeros((8, 128), jnp.float32)
            for t in range(4):
                ends = ends + jnp.where(
                    jnp.logical_and(place >= 4, place + t < 8),
                    EDGE[t] * weight,
                    0.0,
                ) * pltpu.roll(delta, 4 - t, 1)
                ends = ends + jnp.where(
                    jnp.logical_and(place < 4, place >= t),
                    EDGE[t] * weight,
                    0.0,
                ) * pltpu.roll(delta, 124 + t, 1)
            for k in range(16):
                i, t = g * half + k // tiles, k % tiles
                moved = pltpu.roll(ends, (124 - 8 * k) % 128, 1)
                out_ref[f, i, t * 8 : t * 8 + 8, :] += jnp.where(outer, moved, 0.0)
        return carry

    lax.fori_loop(0, fields, span_field, 0, unroll=True)

    when(has_up, down_copy.wait_recv)
    when(has_down, up_copy.wait_recv)
    step_row = row % 4

    def axial_field(f, carry):
        for k in range(cells // 2):
            delta = got_tail[f, k] - ax_tail[f, k]
            ends = (EDGE[0] * weight) * delta
            for t in range(1, 4):
                ends = ends + jnp.where(step_row + t < 4, EDGE[t] * weight, 0.0) * pltpu.roll(
                    delta, 8 - t, 0
                )
            out_ref[f, 2 * k, :8, :] += jnp.where(low_rows, ends, 0.0)
            out_ref[f, 2 * k + 1, :8, :] += jnp.where(low_rows, pltpu.roll(ends, 4, 0), 0.0)
            delta = got_head[f, k] - ax_head[f, k]
            ends = (EDGE[0] * weight) * delta
            for t in range(1, 4):
                ends = ends + jnp.where(step_row >= t, EDGE[t] * weight, 0.0) * pltpu.roll(
                    delta, t, 0
                )
            out_ref[f, 2 * k, rows - 8 :, :] += jnp.where(low_rows, 0.0, pltpu.roll(ends, 4, 0))
            out_ref[f, 2 * k + 1, rows - 8 :, :] += jnp.where(low_rows, 0.0, ends)
        return carry

    lax.fori_loop(0, fields, axial_field, 0, unroll=True)

    for copy in sum_copies:
        copy.wait_send()
    when(has_down, down_copy.wait_send)
    when(has_up, up_copy.wait_send)
    when(has_right, right_copy.wait_send)
    when(has_left, left_copy.wait_send)


def shards(sizes, state, coeffs, lag_shift, harmonics):
    fields, cells, rows, lanes = state.shape
    npitch = sizes[0]
    groups = cells * (rows // 8) // 16
    vmem = lambda *shape: pltpu.VMEM(shape, jnp.float32)
    halo = (fields, cells // 2, 8, lanes)
    packed = (fields, groups, 8, lanes)
    sems = 4 + npitch - 1
    return pl.pallas_call(
        functools.partial(kernel, sizes),
        out_shape=pltpu.VMEM(state.shape, jnp.float32),
        in_specs=[
            pl.BlockSpec(memory_space=pltpu.HBM),
            pl.BlockSpec(memory_space=pltpu.HBM),
            pl.BlockSpec(memory_space=pltpu.HBM),
            pl.BlockSpec(memory_space=pltpu.HBM),
        ],
        out_specs=pl.BlockSpec(memory_space=pltpu.VMEM),
        scratch_shapes=[
            vmem(*state.shape),
            vmem(*coeffs.shape),
            vmem(*state.shape),
            vmem(4, fields, rows, lanes),
            vmem(npitch - 1, 4, fields, rows, lanes),
            vmem(*halo),
            vmem(*halo),
            vmem(*halo),
            vmem(*halo),
            vmem(*packed),
            vmem(*packed),
            vmem(*packed),
            vmem(2, 8, lanes),
            pltpu.VMEM((2 * lanes, lanes), jnp.bfloat16),
            pltpu.SMEM((1,), jnp.int32),
            pltpu.VMEM((1, lanes), jnp.int32),
            pltpu.SemaphoreType.DMA((4,)),
            pltpu.SemaphoreType.DMA((sems,)),
            pltpu.SemaphoreType.DMA((sems,)),
        ],
        compiler_params=pltpu.CompilerParams(collective_id=0, has_side_effects=True),
    )(lag_shift, harmonics.reshape(1, lanes), state, coeffs)


def solution(mesh):
    sizes = tuple(mesh.shape[name] for name in ("pitch", "axial", "span"))
    placed = (
        P(None, "pitch", "axial", "span"),
        P(None, None, None, "axial", "span"),
        P(),
        P("span"),
    )
    return jax.shard_map(
        functools.partial(shards, sizes),
        mesh=mesh,
        in_specs=placed,
        out_specs=P(None, "pitch", "axial", "span"),
        check_vma=False,
    )
```
